32 devices in a mesh: grp: 2 (over y), skill: 16 (over z, x, core).
Axes of the slice: x: 2, y: 2, z: 4, core: 2. Of those that a mesh axis runs over, the one named last changes fastest.
Arguments:
- value_next: bfloat16 [2048, 4, 2048], P('skill', 'grp'), parts along dimension 1, may hold values from -6 to 6
- income_matrix: float32 [64, 32], P('grp'), parts along dimension 0, may hold values from -1 to 1
- block_weights: bfloat16 [16, 16, 4, 128, 128], P('skill')
- block_offset: int32 [16, 16, 4], P('skill'), may hold values from 0 to 3, as said below
- block_count: int32 [16, 16], P('skill'), may hold values from 1 to 4, as said below
- asset_next: int32 [16, 2, 2048], replicated, may hold values from 0 to 1
- flow: float32 [32, 2, 2048], P('grp'), parts along dimension 0, may hold values from -4 to 15
Outputs:
- value_now: bfloat16 [2048, 4, 2048], P('skill', 'grp'), parts along dimension 1
The draws below stay inside these ranges and needn't reach their ends.
There are 2 independent parts, one for each index of `grp`. The reference program is written for one: setup_inputs(seed, part) draws one part's arguments, and reference() takes and returns one part's arrays. A program takes and returns all parts, laid end to end along the dimension named above; an argument that names none is the same for every part. Nothing has to cross between parts.
Inputs may be any that keep to these rules, and one draw needn't show every extreme that they name: `block_offset`: each row of 4 entries is a permutation of 0 to 3, the same for every level. `block_count`: the same for every level.
All inputs are finite; a program needn't handle non-finite values.
Results may differ from the reference program's by a relative error of at most 0.0031.
Values may be sent and summed in bfloat16 or wider, within the bound.
A program may use at most 128 MiB of HBM per device.

```python
import jax
import jax.numpy as jnp
from jax import lax

TILE = 128
H = 64
E = 32
INVEST = 16
BLOCKS = 4
A = 2
TILES = 16
SKILLS = 2048
HE = 2048


def draw_flow(key, part):
    base_key = jax.random.fold_in(key, 11)
    noise_key = jax.random.fold_in(key, 14)
    spread_key = jax.random.fold_in(key, 15)
    shape = (INVEST, A, H * E)
    spread = jnp.exp(jax.random.uniform(spread_key, (1, 1, H * E), jnp.float32, jnp.log(0.005), jnp.log(0.5)))
    base = jnp.clip(jax.random.normal(base_key, (1, A, H * E), jnp.float32), -3.5, 3.5)
    noise = jnp.clip(jax.random.normal(noise_key, shape, jnp.float32), -1.0, 1.0)
    return base + spread * noise


def draw_block_weights(key, part):
    common_key = jax.random.fold_in(key, 21)
    level_key = jax.random.fold_in(key, 22)
    factor = (BLOCKS * TILE) ** (-0.5)
    common = jnp.clip(jax.random.normal(common_key, (TILES, 1, BLOCKS, TILE, TILE), jnp.float32), -6.0, 6.0)
    level = jnp.clip(jax.random.normal(level_key, (TILES, INVEST, BLOCKS, TILE, TILE), jnp.float32), -6.0, 6.0)
    return ((common + 0.075 * level) * factor).astype(jnp.bfloat16)


def draw_block_offset(key, part):
    rank_key = jax.random.fold_in(key, 31)
    ranks = jax.random.randint(rank_key, (TILES, BLOCKS), 0, 1 << 20) * BLOCKS + jnp.arange(BLOCKS, dtype=jnp.int32)[None, :]
    order = jnp.argsort(ranks, axis=-1, stable=True).astype(jnp.int32)
    return jnp.broadcast_to(order[:, None, :], (TILES, INVEST, BLOCKS)).astype(jnp.int32)


def draw_block_count(key, part):
    count_key = jax.random.fold_in(key, 41)
    top_key = jax.random.fold_in(key, 42)
    step_key = jax.random.fold_in(key, 43)
    counts = jax.random.randint(count_key, (TILES,), 1, BLOCKS + 1)
    top_pos = jax.random.randint(top_key, (), 0, TILES)
    low_pos = (top_pos + 1 + jax.random.randint(step_key, (), 0, TILES - 1)) % TILES
    places = jnp.arange(TILES, dtype=jnp.int32)
    counts = jnp.where(places == top_pos, BLOCKS, counts)
    counts = jnp.where(places == low_pos, 1, counts)
    return jnp.broadcast_to(counts[:, None], (TILES, INVEST)).astype(jnp.int32)


def plant(values, key, least, largest):
    index_at = [jax.random.randint(jax.random.fold_in(key, axis), (), 0, length) for axis, length in enumerate(values.shape)]
    widest = values.shape.index(max(values.shape))
    next_to = index_at[:widest] + [(index_at[widest] + 1) % values.shape[widest]] + index_at[widest + 1:]
    return values.at[tuple(index_at)].set(least).at[tuple(next_to)].set(largest)


def shard_levels(own_key, shape, pieces, low, top_value):
    level, own = 1.0, jax.random.fold_in(own_key, 6)
    for dim, parts in pieces:
        steps = jnp.exp(jax.random.uniform(jax.random.fold_in(own, dim), (parts,), jnp.float32, low / len(pieces), top_value / len(pieces)))
        level = level * jnp.repeat(steps, shape[dim] // parts).reshape([-1 if axis == dim else 1 for axis in range(len(shape))])
    return level


def scatter_about(stream_key, dims, width, reach, cuts=(), kind=jnp.bfloat16):
    drawn = width * jax.random.normal(stream_key, dims, jnp.float32)
    if cuts:
        drawn = drawn * shard_levels(stream_key, dims, cuts, -0.22, 0.18)
    return jnp.clip(drawn, -reach, reach).astype(kind)


def setup_inputs(seed: int = 0, part: int = 0) -> dict:
    arg_keys = jax.random.split(jax.random.key(seed), 8)
    part_keys = jax.random.split(jax.random.fold_in(arg_keys[7], part), 8)
    return {
        "value_next": scatter_about(part_keys[0], (HE, A, SKILLS), 1.0, 6.0, ((0, 16),)),
        "income_matrix": scatter_about(part_keys[1], (E, E), E ** -0.5, 1.0, (), jnp.float32),
        "block_weights": draw_block_weights(jax.random.fold_in(arg_keys[7], 71), part),
        "block_offset": draw_block_offset(jax.random.fold_in(arg_keys[7], 71), part),
        "block_count": draw_block_count(jax.random.fold_in(arg_keys[7], 71), part),
        "asset_next": plant(jax.random.randint(arg_keys[5], (INVEST, A, HE), 0, A), jax.random.fold_in(arg_keys[5], 1), 0, A - 1).astype(jnp.int32),
        "flow": draw_flow(jax.random.fold_in(jax.random.fold_in(arg_keys[7], part), 71), part),
    }


def reference(value_next, income_matrix, block_weights, block_offset, block_count, asset_next, flow):
    rows = H * E
    grid = value_next.astype(jnp.float32).reshape(H, E, A * SKILLS)
    mixed = jnp.einsum("fe,hex->hfx", income_matrix, grid, precision=lax.Precision.HIGHEST)
    expected = mixed.reshape(rows, A, SKILLS).astype(jnp.bfloat16)
    padded = jnp.pad(expected, ((0, 0), (0, 0), (0, (BLOCKS - 1) * TILE)))
    place = jnp.arange(BLOCKS, dtype=jnp.int32)
    flow_rows = jnp.transpose(flow, (0, 2, 1))[..., None]
    choose = jnp.transpose(asset_next, (0, 2, 1))

    def one_tile(tile_id):
        start = (tile_id * TILE).astype(jnp.int32)
        window = lax.dynamic_slice_in_dim(padded, start, BLOCKS * TILE, 2).reshape(rows * A, BLOCKS * TILE)
        offsets = block_offset[tile_id]
        counts = block_count[tile_id]
        select = ((offsets[:, :, None] == place[None, None, :]) & (place[None, :, None] < counts[:, None, None])).astype(jnp.float32)
        stacked = jnp.einsum("ikr,ikst->irts", select, block_weights[tile_id].astype(jnp.float32))
        stacked = stacked.astype(jnp.bfloat16).reshape(INVEST, BLOCKS * TILE, TILE)

        def level(index):
            cont = jnp.dot(window, stacked[index], preferred_element_type=jnp.float32).reshape(rows, A, TILE)
            where = jnp.broadcast_to(choose[index][:, :, None], (rows, A, TILE))
            picked = jnp.take_along_axis(cont, where, axis=1)
            return (flow_rows[index] + 0.96 * picked) / 0.05

        scores = lax.map(level, jnp.arange(INVEST, dtype=jnp.int32))
        return (0.05 * jax.nn.logsumexp(scores, axis=0)).astype(jnp.bfloat16)

    result = lax.map(one_tile, jnp.arange(TILES, dtype=jnp.int32))
    return jnp.transpose(result, (1, 2, 0, 3)).reshape(rows, A, SKILLS)
```

```python
import functools
import math

import jax
import jax.numpy as jnp
from jax import lax
from jax.experimental import pallas as pl
from jax.experimental.pallas import tpu as pltpu
from jax.sharding import PartitionSpec as P

def shifted(block, axis, distance):
    devices = range(lax.axis_size(axis))
    route = [(i - distance, i) for i in devices if i - distance in devices]
    return lax.ppermute(block, axis, route)


def on_device_split(
    value_next, income_matrix, block_weights, block_offset, block_count, asset_next, flow
):
    tiles = lax.axis_size("skill")
    local_rows, assets, skills = value_next.shape
    tile = skills // tiles
    rows = local_rows * tiles
    shocks = income_matrix.shape[0]
    parents = rows // shocks
    blocks = block_offset.shape[-1]
    levels = block_offset.shape[1]
    arrived = lax.all_to_all(value_next, "skill", split_axis=2, concat_axis=0, tiled=True)
    width = arrived.shape[2]
    grid = arrived.astype(jnp.float32).reshape(parents, shocks, assets * width)
    mixed = jnp.einsum("fe,hex->hfx", income_matrix, grid, precision=lax.Precision.HIGHEST)
    own_tile = mixed.reshape(rows, assets, width).astype(jnp.bfloat16)
    gathered = [own_tile]
    for step in range(1, blocks):
        gathered.append(shifted(own_tile, "skill", -step))
    window = jnp.concatenate(gathered, axis=2)
    matrix = window.reshape(rows * assets, blocks * tile)
    place = jnp.arange(blocks, dtype=jnp.int32)
    offsets = block_offset[0]
    counts = block_count[0]
    select = (
        (offsets[:, :, None] == place[None, None, :])
        & (place[None, :, None] < counts[:, None, None])
    ).astype(jnp.float32)
    transit = jnp.einsum("ikr,ikst->irts", select, block_weights[0].astype(jnp.float32))
    transit = transit.astype(jnp.bfloat16).reshape(levels, blocks * tile, tile)
    flow_rows = jnp.transpose(flow, (0, 2, 1))[..., None]
    choose = jnp.transpose(asset_next, (0, 2, 1))

    def level_step(index, carry):
        running_max, running_total = carry
        cont = jnp.dot(matrix, transit[index], preferred_element_type=jnp.float32).reshape(
            rows, assets, tile
        )
        chosen = choose[index][:, :, None]
        picked = jnp.zeros((rows, assets, tile), jnp.float32)
        for option in range(assets):
            picked = picked + jnp.where(chosen == option, cont[:, option : option + 1, :], 0.0)
        score = (flow_rows[index] + 0.96 * picked) / 0.05
        new_max = jnp.maximum(running_max, score)
        new_total = running_total * jnp.exp(running_max - new_max) + jnp.exp(score - new_max)
        return (new_max, new_total)

    start_max = jnp.full((rows, assets, tile), -jnp.inf, jnp.float32)
    start_total = jnp.zeros((rows, assets, tile), jnp.float32)
    final_max, final_total = lax.fori_loop(0, levels, level_step, (start_max, start_total))
    value_tile = (0.05 * (final_max + jnp.log(final_total))).astype(jnp.bfloat16)
    return lax.all_to_all(value_tile, "skill", split_axis=0, concat_axis=2, tiled=True)


SUB = 16
STEP = 32
SCALE = math.log2(math.e) / 0.05


def split_three(mix):
    high = mix.astype(jnp.bfloat16)
    rest = mix - high.astype(jnp.float32)
    middle = rest.astype(jnp.bfloat16)
    low = (rest - middle.astype(jnp.float32)).astype(jnp.bfloat16)
    return high, middle, low


def arrange_weights(t, tiles, weights, offsets, counts, sorted_weights):
    levels, blocks, tile, _ = weights.shape

    def one_level(i, carry):
        for r in range(blocks):
            total = jnp.zeros((tile, tile), jnp.float32)
            for k in range(blocks):
                live = (offsets[k] == r) & (counts > k) & (t + r < tiles)
                total = total + jnp.where(live, weights[i, k].astype(jnp.float32), 0.0)
            total = total.astype(jnp.bfloat16)
            for q in range(tile // STEP):
                sorted_weights[q, pl.ds(pl.multiple_of(i * STEP, STEP), STEP), r * tile : (r + 1) * tile] = total[
                    q * STEP : (q + 1) * STEP
                ]
        return carry

    lax.fori_loop(0, levels, one_level, 0)


def one_chunk(window, flow, choose, sorted_weights, scaled, chosen, cont, value, levels, rows):
    for a in range(2):
        scaled[a] = flow[:, a, :] * SCALE
        chosen[a] = choose[:, a, :]
    steps = sorted_weights.shape[0]

    def multiply(q):
        cont[q % 2] = lax.dot_general(
            sorted_weights[q], window, (((1,), (1,)), ((), ())), preferred_element_type=jnp.float32
        )

    def reduce(q):
        for part in range(STEP // SUB):
            for a in range(2):
                scores = []
                for i in range(levels):
                    at = i * STEP + part * SUB
                    first = cont[q % 2, at : at + SUB, :rows]
                    second = cont[q % 2, at : at + SUB, rows:]
                    picked = jnp.where(chosen[a, i : i + 1, :] == 1, second, first)
                    scores.append(scaled[a, i : i + 1, :] + (0.96 * SCALE) * picked)
                top = scores
                while len(top) > 1:
                    top = [jnp.maximum(x, y) for x, y in zip(top[::2], top[1::2])]
                terms = [jnp.exp2(x - top[0]) for x in scores]
                while len(terms) > 1:
                    terms = [x + y for x, y in zip(terms[::2], terms[1::2])]
                start = q * STEP + part * SUB
                value[a, start : start + SUB, :] = (1.0 / SCALE) * (top[0] + jnp.log2(terms[0]))

    multiply(0)
    for q in range(steps):
        if q + 1 < steps:
            multiply(q + 1)
        reduce(q)

MESH = pl.DeviceIdType.MESH


def fused_kernel(
    tiles,
    offsets,
    counts,
    mix,
    values,
    weights,
    flow,
    choose,
    out,
    expected,
    window,
    sorted_weights,
    results,
    scaled,
    chosen,
    cont,
    value,
    base_send,
    base_recv,
    extra_send,
    extra_recv,
    trade_send,
    trade_recv,
    relay_send,
    third_recv,
    out_send,
    out_recv,
    near_sems,
    weight_sems,
    local_sem,
):
    chips = tiles // 2
    planes = chips // 2
    levels, blocks, tile, _ = weights.shape
    rows = values.shape[1]
    me = lax.axis_index("skill")
    chip = lax.div(me, 2)
    core = lax.rem(me, 2)
    partner = chip * 2 + 1 - core
    z = lax.div(chip, 2)
    x = lax.rem(chip, 2)
    high = lax.div(z, planes // 2)
    toward = 1 - 2 * high
    beside = z * 2 + 1 - x

    def device(at):
        return {"skill": at * 2 + core}

    def target_at(step):
        plane = lax.rem(planes // 2 - high + toward * lax.div(step, 2) + planes, planes)
        return plane, plane * 2 + lax.rem(x + step, 2)

    def source_at(step):
        plane = lax.rem(z + toward * (1 + lax.div(step, 2)) + planes, planes)
        return plane, plane * 2 + lax.rem(step, 2)

    barrier = pltpu.get_barrier_semaphore()

    def greet(step, carry):
        at = lax.rem(chip + step, chips)
        pl.semaphore_signal(barrier, inc=1, device_id=device(at), device_id_type=MESH)
        return carry

    lax.fori_loop(1, chips, greet, 0)
    pl.semaphore_signal(barrier, inc=1, device_id={"skill": partner}, device_id_type=MESH)

    parts = split_three(mix[...])

    def mixed(target, a):
        block = values[a, :, pl.ds(pl.multiple_of(target * 2 * tile, 2 * tile), 2 * tile)]
        total = jnp.dot(parts[2], block, preferred_element_type=jnp.float32)
        total = total + jnp.dot(parts[1], block, preferred_element_type=jnp.float32)
        total = total + jnp.dot(parts[0], block, preferred_element_type=jnp.float32)
        return total.astype(jnp.bfloat16)

    def remote(source, target, send, recv, at):
        return pltpu.make_async_remote_copy(
            src_ref=source,
            dst_ref=target,
            send_sem=send,
            recv_sem=recv,
            device_id=device(at),
            device_id_type=MESH,
        )

    def base_copy(target, origin):
        return remote(
            expected.at[pl.ds(target * 2, 2)],
            window.at[origin, pl.ds(0, 2)],
            base_send.at[target],
            base_recv.at[origin],
            target,
        )

    def left_extra(target, origin):
        return remote(
            expected.at[target * 2 + 4],
            window.at[origin, 4],
            extra_send.at[target],
            extra_recv.at[origin],
            target,
        )

    def right_extra(target, origin):
        return remote(
            expected.at[pl.ds(target * 2 + 3, 2)],
            window.at[origin, pl.ds(3, 2)],
            extra_send.at[target],
            extra_recv.at[origin],
            target,
        )

    def near_copy(origin):
        return remote(
            expected.at[pl.ds(beside * 2, blocks + 1)],
            window.at[origin],
            near_sems.at[0],
            near_sems.at[1],
            beside,
        )

    def trade_right(at):
        return remote(
            window.at[at, 4], window.at[at, 2], trade_send.at[at], trade_recv.at[at], beside
        )

    def trade_left(at):
        return remote(
            window.at[at, pl.ds(0, 2)],
            window.at[at, pl.ds(2, 2)],
            trade_send.at[at],
            trade_recv.at[at],
            beside,
        )

    below = lax.rem(z + planes - 1, planes) * 2

    def relay_first(at):
        return remote(
            window.at[at, 0], window.at[at, 4], relay_send.at[0, at], extra_recv.at[at], below
        )

    def relay_second(at):
        return remote(
            window.at[at, 1], window.at[at, 3], relay_send.at[1, at], extra_recv.at[at], below + 1
        )

    def relay_third(at):
        return remote(
            window.at[at, 0], window.at[at, 4], relay_send.at[0, at], third_recv.at[at], below + 1
        )

    def out_copy(target, origin):
        return remote(
            results.at[target],
            out.at[pl.ds(origin * 2, 2)],
            out_send.at[target],
            out_recv.at[origin],
            target,
        )

    def weight_copy(which):
        return pltpu.make_async_remote_copy(
            src_ref=sorted_weights.at[which],
            dst_ref=sorted_weights.at[which],
            send_sem=weight_sems.at[0],
            recv_sem=weight_sems.at[1],
            device_id={"skill": partner},
            device_id_type=MESH,
        )

    pl.semaphore_wait(barrier, chips)

    for r in range(blocks - 1):
        expected[tiles + r] = jnp.zeros(expected.shape[1:], jnp.bfloat16)

    def send_in(step, carry):
        plane, target = target_at(step)
        for a in range(2):
            total = mixed(target, a)
            expected[target * 2, a] = total[:, :tile]
            expected[target * 2 + 1, a] = total[:, tile:]

        @pl.when(plane != z)
        def _():
            base_copy(target, chip).start()

        return carry

    lax.fori_loop(0, chips, send_in, 0)
    near_copy(chip).start()

    def each_extra(plane, target, act):
        right = lax.rem(target, 2)
        wanted = (plane != z) & (plane + 1 < planes) & (z <= plane + 1)

        @pl.when(wanted & (right == 0))
        def _():
            act(left_extra(target, chip))

        @pl.when(wanted & (right == 1))
        def _():
            act(right_extra(target, chip))

    def send_extra(step, carry):
        plane, target = target_at(step)
        each_extra(plane, target, lambda copy: copy.start())
        return carry

    lax.fori_loop(0, chips, send_extra, 0)
    for r in range(blocks + 1):
        window[chip, r] = expected[chip * 2 + r]

    last = z + 1 >= planes

    @pl.when(last)
    def _():
        def clear(step, carry):
            _, at = source_at(step)
            window[at, 4] = jnp.zeros(window.shape[2:], jnp.bfloat16)

            @pl.when(x == 1)
            def _():
                for slot in (2, 3):
                    window[at, slot] = jnp.zeros(window.shape[2:], jnp.bfloat16)

            return carry

        lax.fori_loop(0, chips - 2, clear, 0)

    arrange_weights(
        me, tiles, weights, [offsets[0, k] for k in range(blocks)], counts[0, 0], sorted_weights.at[core]
    )
    weight_copy(core).start()

    def each_passed(plane, at, act):
        @pl.when(x == 1)
        def _():
            act(trade_left(at))

        passed = (plane > z) & (z >= 1)

        @pl.when(passed & (x == 0))
        def _():
            act(relay_first(at))
            act(relay_second(at))

        @pl.when(passed & (x == 1))
        def _():
            act(relay_third(at))

    def arrive(step):
        plane, at = source_at(step)
        base_copy(chip, at).wait_recv()
        each_passed(plane, at, lambda copy: copy.start())

        @pl.when((x == 0) & jnp.logical_not(last))
        def _():
            left_extra(chip, at).wait_recv()
            trade_right(at).start()

    def ready(step):
        plane, at = source_at(step)

        @pl.when(x == 0)
        def _():
            trade_left(at).wait_recv()

        @pl.when((x == 1) & jnp.logical_not(last))
        def _():
            trade_right(at).wait_recv()

            @pl.when(plane <= z + 1)
            def _():
                right_extra(chip, at).wait_recv()

            @pl.when(plane > z + 1)
            def _():
                relay_second(at).wait_recv()
                relay_third(at).wait_recv()

    def compute(at):
        start = pl.multiple_of((at * 2 + core) * rows, rows)
        flow_here = flow[:, :, pl.ds(start, rows)]
        choose_here = choose[:, :, pl.ds(start, rows)]

        def one_tile(t, inner):
            blocks_here = [window[at, t + r].reshape(2 * rows, tile) for r in range(blocks)]
            one_chunk(
                jnp.concatenate(blocks_here, axis=1),
                flow_here,
                choose_here,
                sorted_weights.at[t],
                scaled,
                chosen,
                cont,
                value,
                levels,
                rows,
            )
            for a in range(2):
                results[at, t, a] = value[a].T.astype(jnp.bfloat16)
            return inner

        lax.fori_loop(0, 2, one_tile, 0)

    weight_copy(1 - core).wait_recv()

    def advance(step, carry):
        distant = lax.max(step - 2, 0)
        _, far = source_at(distant)
        same = lax.max(1 - step, 0)
        next_to = lax.max(1 - lax.max(step - 1, 1 - step), 0)
        at = same * chip + next_to * beside + (1 - same - next_to) * far

        @pl.when(step == 1)
        def _():
            near_copy(beside).wait_recv()

        @pl.when(step >= 2)
        def _():
            ready(distant)

        compute(at)

        @pl.when(step >= 1)
        def _():
            out_copy(at, chip).start()

        @pl.when(step == 0)
        def _():
            pltpu.make_async_copy(results.at[chip], out.at[pl.ds(chip * 2, 2)], local_sem).start()

        @pl.when(step + 2 < chips)
        def _():
            arrive(step)

        return carry

    lax.fori_loop(0, chips, advance, 0)

    pltpu.make_async_copy(results.at[chip], out.at[pl.ds(chip * 2, 2)], local_sem).wait()
    weight_copy(core).wait_send()
    near_copy(chip).wait_send()

    def finish(step, carry):
        plane, target = target_at(step)

        @pl.when(plane != z)
        def _():
            base_copy(target, chip).wait_send()

        each_extra(plane, target, lambda copy: copy.wait_send())

        @pl.when(target != chip)
        def _():
            out_copy(target, chip).wait_send()
            out_copy(target, target).wait_recv()

        return carry

    lax.fori_loop(0, chips, finish, 0)

    def passed_on(step, carry):
        plane, at = source_at(step)
        each_passed(plane, at, lambda copy: copy.wait_send())

        @pl.when((x == 0) & jnp.logical_not(last))
        def _():
            trade_right(at).wait_send()

        return carry

    lax.fori_loop(0, chips - 2, passed_on, 0)


def on_device(value_next, income_matrix, block_weights, block_offset, block_count, asset_next, flow):
    tiles = lax.axis_size("skill")
    chips = tiles // 2
    rows, assets, skills = value_next.shape
    tile = skills // tiles
    shocks = income_matrix.shape[0]
    levels, blocks = block_weights.shape[1:3]
    mix = jnp.kron(jnp.eye(rows // shocks, dtype=jnp.float32), income_matrix)
    turned = jnp.transpose(value_next, (1, 0, 2))
    smem = pl.BlockSpec(memory_space=pltpu.SMEM)
    vmem = pl.BlockSpec(memory_space=pltpu.VMEM)
    dma = pltpu.SemaphoreType.DMA
    back = pl.pallas_call(
        functools.partial(fused_kernel, tiles),
        out_shape=jax.ShapeDtypeStruct((tiles, assets, rows, tile), jnp.bfloat16),
        in_specs=[smem, smem, vmem, vmem, vmem, vmem, vmem],
        out_specs=pl.BlockSpec(memory_space=pl.ANY),
        scratch_shapes=[
            pltpu.VMEM((tiles + blocks - 1, assets, rows, tile), jnp.bfloat16),
            pltpu.VMEM((chips, blocks + 1, assets, rows, tile), jnp.bfloat16),
            pltpu.VMEM((2, tile // STEP, levels * STEP, blocks * tile), jnp.bfloat16),
            pltpu.VMEM((chips, 2, assets, rows, tile), jnp.bfloat16),
            pltpu.VMEM((assets, levels, rows), jnp.float32),
            pltpu.VMEM((assets, levels, rows), jnp.int32),
            pltpu.VMEM((2, levels * STEP, assets * rows), jnp.float32),
            pltpu.VMEM((assets, tile, rows), jnp.float32),
            dma((chips,)),
            dma((chips,)),
            dma((chips,)),
            dma((chips,)),
            dma((chips,)),
            dma((chips,)),
            dma((2, chips)),
            dma((chips,)),
            dma((chips,)),
            dma((chips,)),
            dma((2,)),
            dma((2,)),
            dma,
        ],
        compiler_params=pltpu.CompilerParams(
            collective_id=0, has_side_effects=True, vmem_limit_bytes=48 * 1024 * 1024
        ),
    )(block_offset[0], block_count, mix, turned, block_weights[0], flow, asset_next)
    return jnp.transpose(back, (2, 1, 0, 3)).reshape(rows, assets, skills)


def solution(mesh):
    placed = (
        P("skill", "grp", None),
        P("grp", None),
        P("skill", None, None, None, None),
        P("skill", None, None),
        P("skill", None),
        P(),
        P("grp", None, None),
    )

    def body(value_next, income_matrix, *rest):
        whole = value_next.shape[0] % income_matrix.shape[0] == 0 and mesh.shape["skill"] % 8 == 0
        return (on_device if whole else on_device_split)(value_next, income_matrix, *rest)

    return jax.shard_map(
        body, mesh=mesh, in_specs=placed, out_specs=P("skill", "grp", None), check_vma=False
    )
```

```python
import functools
import math

import jax
import jax.numpy as jnp
from jax import lax
from jax.experimental import pallas as pl
from jax.experimental.pallas import tpu as pltpu
from jax.sharding import PartitionSpec as P

def shifted(block, axis, distance):
    devices = range(lax.axis_size(axis))
    route = [(i - distance, i) for i in devices if i - distance in devices]
    return lax.ppermute(block, axis, route)


def on_device_split(
    value_next, income_matrix, block_weights, block_offset, block_count, asset_next, flow
):
    tiles = lax.axis_size("skill")
    local_rows, assets, skills = value_next.shape
    tile = skills // tiles
    rows = local_rows * tiles
    shocks = income_matrix.shape[0]
    parents = rows // shocks
    blocks = block_offset.shape[-1]
    levels = block_offset.shape[1]
    arrived = lax.all_to_all(value_next, "skill", split_axis=2, concat_axis=0, tiled=True)
    width = arrived.shape[2]
    grid = arrived.astype(jnp.float32).reshape(parents, shocks, assets * width)
    mixed = jnp.einsum("fe,hex->hfx", income_matrix, grid, precision=lax.Precision.HIGHEST)
    own_tile = mixed.reshape(rows, assets, width).astype(jnp.bfloat16)
    gathered = [own_tile]
    for step in range(1, blocks):
        gathered.append(shifted(own_tile, "skill", -step))
    window = jnp.concatenate(gathered, axis=2)
    matrix = window.reshape(rows * assets, blocks * tile)
    place = jnp.arange(blocks, dtype=jnp.int32)
    offsets = block_offset[0]
    counts = block_count[0]
    select = (
        (offsets[:, :, None] == place[None, None, :])
        & (place[None, :, None] < counts[:, None, None])
    ).astype(jnp.float32)
    transit = jnp.einsum("ikr,ikst->irts", select, block_weights[0].astype(jnp.float32))
    transit = transit.astype(jnp.bfloat16).reshape(levels, blocks * tile, tile)
    flow_rows = jnp.transpose(flow, (0, 2, 1))[..., None]
    choose = jnp.transpose(asset_next, (0, 2, 1))

    def level_step(index, carry):
        running_max, running_total = carry
        cont = jnp.dot(matrix, transit[index], preferred_element_type=jnp.float32).reshape(
            rows, assets, tile
        )
        chosen = choose[index][:, :, None]
        picked = jnp.zeros((rows, assets, tile), jnp.float32)
        for option in range(assets):
            picked = picked + jnp.where(chosen == option, cont[:, option : option + 1, :], 0.0)
        score = (flow_rows[index] + 0.96 * picked) / 0.05
        new_max = jnp.maximum(running_max, score)
        new_total = running_total * jnp.exp(running_max - new_max) + jnp.exp(score - new_max)
        return (new_max, new_total)

    start_max = jnp.full((rows, assets, tile), -jnp.inf, jnp.float32)
    start_total = jnp.zeros((rows, assets, tile), jnp.float32)
    final_max, final_total = lax.fori_loop(0, levels, level_step, (start_max, start_total))
    value_tile = (0.05 * (final_max + jnp.log(final_total))).astype(jnp.bfloat16)
    return lax.all_to_all(value_tile, "skill", split_axis=0, concat_axis=2, tiled=True)


SUB = 16
STEP = 32
SCALE = math.log2(math.e) / 0.05


def split_three(mix):
    high = mix.astype(jnp.bfloat16)
    rest = mix - high.astype(jnp.float32)
    middle = rest.astype(jnp.bfloat16)
    low = (rest - middle.astype(jnp.float32)).astype(jnp.bfloat16)
    return high, middle, low


def arrange_weights(t, tiles, weights, offsets, counts, sorted_weights):
    levels, blocks, tile, _ = weights.shape

    def one_level(i, carry):
        for r in range(blocks):
            total = jnp.zeros((tile, tile), jnp.float32)
            for k in range(blocks):
                live = (offsets[k] == r) & (counts > k) & (t + r < tiles)
                total = total + jnp.where(live, weights[i, k].astype(jnp.float32), 0.0)
            total = total.astype(jnp.bfloat16)
            for q in range(tile // STEP):
                sorted_weights[q, pl.ds(pl.multiple_of(i * STEP, STEP), STEP), r * tile : (r + 1) * tile] = total[
                    q * STEP : (q + 1) * STEP
                ]
        return carry

    lax.fori_loop(0, levels, one_level, 0)


def one_chunk(window, flow, choose, sorted_weights, scaled, chosen, cont, value, levels, rows):
    for a in range(2):
        scaled[a] = flow[:, a, :] * SCALE
        chosen[a] = choose[:, a, :]
    steps = sorted_weights.shape[0]

    def multiply(q):
        cont[q % 2] = lax.dot_general(
            sorted_weights[q], window, (((1,), (1,)), ((), ())), preferred_element_type=jnp.float32
        )

    def reduce(q):
        for part in range(STEP // SUB):
            for a in range(2):
                scores = []
                for i in range(levels):
                    at = i * STEP + part * SUB
                    first = cont[q % 2, at : at + SUB, :rows]
                    second = cont[q % 2, at : at + SUB, rows:]
                    picked = jnp.where(chosen[a, i : i + 1, :] == 1, second, first)
                    scores.append(scaled[a, i : i + 1, :] + (0.96 * SCALE) * picked)
                top = scores
                while len(top) > 1:
                    top = [jnp.maximum(x, y) for x, y in zip(top[::2], top[1::2])]
                terms = [jnp.exp2(x - top[0]) for x in scores]
                while len(terms) > 1:
                    terms = [x + y for x, y in zip(terms[::2], terms[1::2])]
                start = q * STEP + part * SUB
                value[a, start : start + SUB, :] = (1.0 / SCALE) * (top[0] + jnp.log2(terms[0]))

    multiply(0)
    for q in range(steps):
        if q + 1 < steps:
            multiply(q + 1)
        reduce(q)

MESH = pl.DeviceIdType.MESH


def pick(index, table):
    chosen = table[0]
    for at, entry in enumerate(table[1:], 1):
        chosen = jnp.where(index == at, entry, chosen)
    return chosen


ARRIVE = ((1, 3, 2), (3, 2, 0), (0, 3, 1), (2, 0, 1))
WORK = ((1, 3, 2), (2, 0, 3), (0, 3, 1), (2, 0, 1))
SEND = ((2, 3, 1), (2, 3, 0), (1, 0, 3), (1, 0, 2))
PIECES = 4


def fused_kernel(
    tiles,
    offsets,
    counts,
    mix,
    values,
    weights,
    flow,
    choose,
    out,
    expected,
    window,
    sorted_weights,
    results,
    scaled,
    chosen,
    cont,
    value,
    base_send,
    base_recv,
    relay_send,
    extra_recv,
    out_send,
    out_recv,
    across_send,
    across_recv,
    over_send,
    over_recv,
    core_send,
    core_recv,
    local_sems,
):
    planes = len(SEND)
    levels, blocks, tile, _ = weights.shape
    rows = values.shape[1]
    near = tiles // planes
    reach = near + blocks - 1
    me = lax.axis_index("skill")
    y = lax.axis_index("grp")
    z = lax.div(me, 4)
    x = lax.rem(lax.div(me, 2), 2)
    core = lax.rem(me, 2)
    last = z + 1 >= planes

    def column(plane):
        return {"skill": plane * 4 + x * 2 + core}

    across = {"skill": z * 4 + (1 - x) * 2 + core}
    over = {"grp": 1 - y}
    partner = {"skill": z * 4 + x * 2 + 1 - core}

    barrier = pltpu.get_barrier_semaphore()
    for step in range(1, planes):
        pl.semaphore_signal(
            barrier, inc=1, device_id=column(lax.rem(z + step, planes)), device_id_type=MESH
        )
    for other in (across, over, partner):
        pl.semaphore_signal(barrier, inc=1, device_id=other, device_id_type=MESH)

    parts = split_three(mix[...])

    def mix_pair(pair, carry):
        for a in range(2):
            block = values[a, :, pl.ds(pl.multiple_of(pair * 2 * tile, 2 * tile), 2 * tile)]
            total = jnp.dot(parts[2], block, preferred_element_type=jnp.float32)
            total = total + jnp.dot(parts[1], block, preferred_element_type=jnp.float32)
            total = total + jnp.dot(parts[0], block, preferred_element_type=jnp.float32)
            total = total.astype(jnp.bfloat16)
            expected[pair * 2, a] = total[:, :tile]
            expected[pair * 2 + 1, a] = total[:, tile:]
        return carry

    lax.fori_loop(0, tiles // 2, mix_pair, 0)
    for r in range(blocks - 1):
        expected[tiles + r] = jnp.zeros(expected.shape[1:], jnp.bfloat16)

    def remote(source, target, send, recv, device):
        return pltpu.make_async_remote_copy(
            src_ref=source,
            dst_ref=target,
            send_sem=send,
            recv_sem=recv,
            device_id=device,
            device_id_type=MESH,
        )

    def base_copy(plane, origin, count):
        return remote(
            expected.at[pl.ds(plane * near, count)],
            window.at[origin, pl.ds(0, count)],
            base_send.at[plane],
            base_recv.at[origin],
            column(plane),
        )

    def each_base(origin, plane, act):
        wide = (plane + 1 >= origin) & (plane + 1 < planes)

        @pl.when(wide)
        def _():
            act(base_copy(plane, origin, reach))

        @pl.when(jnp.logical_not(wide))
        def _():
            act(base_copy(plane, origin, near))

    def relay_copy(origin):
        return remote(
            window.at[origin, pl.ds(0, blocks - 1)],
            window.at[origin, pl.ds(near, blocks - 1)],
            relay_send.at[origin],
            extra_recv.at[origin],
            column(lax.rem(z + planes - 1, planes)),
        )

    def out_copy(side, plane, origin):
        pair = lax.rem(x + side, 2) * 2
        return remote(
            results.at[plane, pl.ds(pair, 2)],
            out.at[pl.ds(origin * near + pair, 2)],
            out_send.at[side, plane],
            out_recv.at[side, origin],
            column(plane),
        )

    def keep_copy(side):
        pair = lax.rem(x + side, 2) * 2
        return pltpu.make_async_copy(
            results.at[z, pl.ds(pair, 2)], out.at[pl.ds(z * near + pair, 2)], local_sems.at[side]
        )

    steps = sorted_weights.shape[1]
    part = sorted_weights.shape[2] * (steps // 2) // PIECES
    per_step = sorted_weights.shape[2] // part

    def piece(which, half, index):
        return sorted_weights.at[
            which, half * (steps // 2) + index // per_step, pl.ds(index % per_step * part, part)
        ]

    mine = x * 2 + core
    foreign = (1 - x) * 2 + core

    def across_copy(which, index):
        ref = piece(which, y, index)
        return remote(ref, ref, across_send.at[index], across_recv.at[index], across)

    def over_copy(half, index):
        ref = piece(foreign, half, index)
        return remote(ref, ref, over_send.at[index], over_recv.at[index], over)

    def own_copy(which):
        ref = sorted_weights.at[which]
        return remote(ref, ref, core_send.at[2], core_recv.at[2], partner)

    def half_copy(which, half, index):
        ref = sorted_weights.at[which, pl.ds(half * (steps // 2), steps // 2)]
        return remote(ref, ref, core_send.at[index], core_recv.at[index], partner)

    pl.semaphore_wait(barrier, planes + 2)

    for step in range(planes - 1):
        each_base(z, pick(z, [order[step] for order in SEND]), lambda copy: copy.start())

    arrange_weights(
        me, tiles, weights, [offsets[0, k] for k in range(blocks)], counts[0, 0], sorted_weights.at[mine]
    )
    for index in range(PIECES):
        across_copy(mine, index).start()
    own_copy(mine).start()

    for r in range(reach):
        window[z, r] = expected[z * near + r]

    @pl.when(last)
    def _():
        for step in range(1, planes):
            for r in range(near, reach):
                window[lax.rem(z + step, planes), r] = jnp.zeros(window.shape[2:], jnp.bfloat16)

    def arrive(order):
        origin = pick(z, order)
        each_base(origin, z, lambda copy: copy.wait_recv())

        @pl.when((origin > z) & (z >= 1))
        def _():
            relay_copy(origin).start()

    def hand_on(index):
        across_copy(foreign, index).wait_recv()
        over_copy(y, index).start()

    def compute(origin, side):
        start = pl.multiple_of((origin * 4 + x * 2 + core) * rows, rows)
        flow_here = flow[:, :, pl.ds(start, rows)]
        choose_here = choose[:, :, pl.ds(start, rows)]
        first = lax.rem(x + side, 2) * 2

        def one_tile(t, inner):
            blocks_here = [window[origin, t + r].reshape(2 * rows, tile) for r in range(blocks)]
            one_chunk(
                jnp.concatenate(blocks_here, axis=1),
                flow_here,
                choose_here,
                sorted_weights.at[t],
                scaled,
                chosen,
                cont,
                value,
                levels,
                rows,
            )
            for a in range(2):
                results[origin, t, a] = value[a].T.astype(jnp.bfloat16)
            return inner

        lax.fori_loop(first, first + 2, one_tile, 0)

    own_copy(x * 2 + 1 - core).wait_recv()

    def advance(step, carry):
        side = lax.div(step, planes)
        turn = lax.rem(step + planes - 1 + side, planes)
        origin = jnp.where(turn == planes - 1, z, 0)
        for at in range(planes - 1):
            origin = jnp.where(turn == at, pick(z, [order[at] for order in WORK]), origin)

        @pl.when(step == 1)
        def _():
            arrive([order[0] for order in ARRIVE])
            hand_on(0)
            hand_on(1)
            arrive([order[1] for order in ARRIVE])

        @pl.when(step == 2)
        def _():
            hand_on(2)
            hand_on(3)
            half_copy(foreign, y, 0).start()
            arrive([order[2] for order in ARRIVE])

        @pl.when(step == 3)
        def _():
            for index in range(PIECES):
                over_copy(1 - y, index).wait_recv()
            half_copy(foreign, 1 - y, 1).start()

        @pl.when(step == planes)
        def _():
            half_copy((1 - x) * 2 + 1 - core, y, 0).wait_recv()
            half_copy((1 - x) * 2 + 1 - core, 1 - y, 1).wait_recv()

        @pl.when((side == 0) & (origin > z + 1))
        def _():
            relay_copy(origin).wait_recv()

        compute(origin, side)

        @pl.when(origin != z)
        def _():
            out_copy(side, origin, z).start()

        @pl.when(origin == z)
        def _():
            keep_copy(side).start()

        return carry

    lax.fori_loop(0, 2 * planes, advance, 0)

    for side in range(2):
        keep_copy(side).wait()
    own_copy(mine).wait_send()
    half_copy(foreign, y, 0).wait_send()
    half_copy(foreign, 1 - y, 1).wait_send()
    for index in range(PIECES):
        across_copy(mine, index).wait_send()
        over_copy(y, index).wait_send()

    def finish(step, carry):
        plane = lax.rem(z + step, planes)
        each_base(z, plane, lambda copy: copy.wait_send())

        @pl.when((plane > z) & (z >= 1))
        def _():
            relay_copy(plane).wait_send()

        for side in range(2):
            out_copy(side, plane, z).wait_send()
            out_copy(side, plane, plane).wait_recv()
        return carry

    lax.fori_loop(1, planes, finish, 0)


def on_device(value_next, income_matrix, block_weights, block_offset, block_count, asset_next, flow):
    tiles = lax.axis_size("skill")
    planes = len(SEND)
    rows, assets, skills = value_next.shape
    tile = skills // tiles
    shocks = income_matrix.shape[0]
    levels, blocks = block_weights.shape[1:3]
    mix = jnp.kron(jnp.eye(rows // shocks, dtype=jnp.float32), income_matrix)
    turned = jnp.transpose(value_next, (1, 0, 2))
    smem = pl.BlockSpec(memory_space=pltpu.SMEM)
    vmem = pl.BlockSpec(memory_space=pltpu.VMEM)
    dma = pltpu.SemaphoreType.DMA
    back = pl.pallas_call(
        functools.partial(fused_kernel, tiles),
        out_shape=jax.ShapeDtypeStruct((tiles, assets, rows, tile), jnp.bfloat16),
        in_specs=[smem, smem, vmem, vmem, vmem, vmem, vmem],
        out_specs=pl.BlockSpec(memory_space=pl.ANY),
        scratch_shapes=[
            pltpu.VMEM((tiles + blocks - 1, assets, rows, tile), jnp.bfloat16),
            pltpu.VMEM((planes, tiles // planes + blocks - 1, assets, rows, tile), jnp.bfloat16),
            pltpu.VMEM((4, tile // STEP, levels * STEP, blocks * tile), jnp.bfloat16),
            pltpu.VMEM((planes, tiles // planes, assets, rows, tile), jnp.bfloat16),
            pltpu.VMEM((assets, levels, rows), jnp.float32),
            pltpu.VMEM((assets, levels, rows), jnp.int32),
            pltpu.VMEM((2, levels * STEP, assets * rows), jnp.float32),
            pltpu.VMEM((assets, tile, rows), jnp.float32),
            dma((planes,)),
            dma((planes,)),
            dma((planes,)),
            dma((planes,)),
            dma((2, planes)),
            dma((2, planes)),
            dma((PIECES,)),
            dma((PIECES,)),
            dma((PIECES,)),
            dma((PIECES,)),
            dma((3,)),
            dma((3,)),
            dma((2,)),
        ],
        compiler_params=pltpu.CompilerParams(
            collective_id=0, has_side_effects=True, vmem_limit_bytes=48 * 1024 * 1024
        ),
    )(block_offset[0], block_count, mix, turned, block_weights[0], flow, asset_next)
    return jnp.transpose(back, (2, 1, 0, 3)).reshape(rows, assets, skills)


def solution(mesh):
    placed = (
        P("skill", "grp", None),
        P("grp", None),
        P("skill", None, None, None, None),
        P("skill", None, None),
        P("skill", None),
        P(),
        P("grp", None, None),
    )

    def body(value_next, income_matrix, *rest):
        whole = value_next.shape[0] % income_matrix.shape[0] == 0
        whole = whole and mesh.shape["skill"] == 4 * len(SEND) and mesh.shape["grp"] == 2
        return (on_device if whole else on_device_split)(value_next, income_matrix, *rest)

    return jax.shard_map(
        body, mesh=mesh, in_specs=placed, out_specs=P("skill", "grp", None), check_vma=False
    )
```

```python
import functools
import math

import jax
import jax.numpy as jnp
from jax import lax
from jax.experimental import pallas as pl
from jax.experimental.pallas import tpu as pltpu
from jax.sharding import PartitionSpec as P

def shifted(block, axis, distance):
    devices = range(lax.axis_size(axis))
    route = [(i - distance, i) for i in devices if i - distance in devices]
    return lax.ppermute(block, axis, route)


def on_device_split(
    value_next, income_matrix, block_weights, block_offset, block_count, asset_next, flow
):
    tiles = lax.axis_size("skill")
    local_rows, assets, skills = value_next.shape
    tile = skills // tiles
    rows = local_rows * tiles
    shocks = income_matrix.shape[0]
    parents = rows // shocks
    blocks = block_offset.shape[-1]
    levels = block_offset.shape[1]
    arrived = lax.all_to_all(value_next, "skill", split_axis=2, concat_axis=0, tiled=True)
    width = arrived.shape[2]
    grid = arrived.astype(jnp.float32).reshape(parents, shocks, assets * width)
    mixed = jnp.einsum("fe,hex->hfx", income_matrix, grid, precision=lax.Precision.HIGHEST)
    own_tile = mixed.reshape(rows, assets, width).astype(jnp.bfloat16)
    gathered = [own_tile]
    for step in range(1, blocks):
        gathered.append(shifted(own_tile, "skill", -step))
    window = jnp.concatenate(gathered, axis=2)
    matrix = window.reshape(rows * assets, blocks * tile)
    place = jnp.arange(blocks, dtype=jnp.int32)
    offsets = block_offset[0]
    counts = block_count[0]
    select = (
        (offsets[:, :, None] == place[None, None, :])
        & (place[None, :, None] < counts[:, None, None])
    ).astype(jnp.float32)
    transit = jnp.einsum("ikr,ikst->irts", select, block_weights[0].astype(jnp.float32))
    transit = transit.astype(jnp.bfloat16).reshape(levels, blocks * tile, tile)
    flow_rows = jnp.transpose(flow, (0, 2, 1))[..., None]
    choose = jnp.transpose(asset_next, (0, 2, 1))

    def level_step(index, carry):
        running_max, running_total = carry
        cont = jnp.dot(matrix, transit[index], preferred_element_type=jnp.float32).reshape(
            rows, assets, tile
        )
        chosen = choose[index][:, :, None]
        picked = jnp.zeros((rows, assets, tile), jnp.float32)
        for option in range(assets):
            picked = picked + jnp.where(chosen == option, cont[:, option : option + 1, :], 0.0)
        score = (flow_rows[index] + 0.96 * picked) / 0.05
        new_max = jnp.maximum(running_max, score)
        new_total = running_total * jnp.exp(running_max - new_max) + jnp.exp(score - new_max)
        return (new_max, new_total)

    start_max = jnp.full((rows, assets, tile), -jnp.inf, jnp.float32)
    start_total = jnp.zeros((rows, assets, tile), jnp.float32)
    final_max, final_total = lax.fori_loop(0, levels, level_step, (start_max, start_total))
    value_tile = (0.05 * (final_max + jnp.log(final_total))).astype(jnp.bfloat16)
    return lax.all_to_all(value_tile, "skill", split_axis=0, concat_axis=2, tiled=True)


SUB = 16
STEP = 32
SCALE = math.log2(math.e) / 0.05


def split_three(mix):
    high = mix.astype(jnp.bfloat16)
    rest = mix - high.astype(jnp.float32)
    middle = rest.astype(jnp.bfloat16)
    low = (rest - middle.astype(jnp.float32)).astype(jnp.bfloat16)
    return high, middle, low


def arrange_weights(t, tiles, weights, offsets, counts, sorted_weights):
    levels, blocks, tile, _ = weights.shape

    def one_level(i, carry):
        for r in range(blocks):
            total = jnp.zeros((tile, tile), jnp.float32)
            for k in range(blocks):
                live = (offsets[k] == r) & (counts > k) & (t + r < tiles)
                total = total + jnp.where(live, weights[i, k].astype(jnp.float32), 0.0)
            total = total.astype(jnp.bfloat16)
            for q in range(tile // STEP):
                sorted_weights[q, pl.ds(pl.multiple_of(i * STEP, STEP), STEP), r * tile : (r + 1) * tile] = total[
                    q * STEP : (q + 1) * STEP
                ]
        return carry

    lax.fori_loop(0, levels, one_level, 0)


def one_chunk(window, flow, choose, sorted_weights, scaled, chosen, cont, value, levels, rows):
    for a in range(2):
        scaled[a] = flow[:, a, :] * SCALE
        chosen[a] = choose[:, a, :]
    steps = sorted_weights.shape[0]

    def multiply(q):
        cont[q % 2] = lax.dot_general(
            sorted_weights[q], window, (((1,), (1,)), ((), ())), preferred_element_type=jnp.float32
        )

    def reduce(q):
        for part in range(STEP // SUB):
            for a in range(2):
                scores = []
                for i in range(levels):
                    at = i * STEP + part * SUB
                    first = cont[q % 2, at : at + SUB, :rows]
                    second = cont[q % 2, at : at + SUB, rows:]
                    picked = jnp.where(chosen[a, i : i + 1, :] == 1, second, first)
                    scores.append(scaled[a, i : i + 1, :] + (0.96 * SCALE) * picked)
                top = scores
                while len(top) > 1:
                    top = [jnp.maximum(x, y) for x, y in zip(top[::2], top[1::2])]
                terms = [jnp.exp2(x - top[0]) for x in scores]
                while len(terms) > 1:
                    terms = [x + y for x, y in zip(terms[::2], terms[1::2])]
                start = q * STEP + part * SUB
                value[a, start : start + SUB, :] = (1.0 / SCALE) * (top[0] + jnp.log2(terms[0]))

    multiply(0)
    for q in range(steps):
        if q + 1 < steps:
            multiply(q + 1)
        reduce(q)

MESH = pl.DeviceIdType.MESH


def pick(index, table):
    chosen = table[0]
    for at, entry in enumerate(table[1:], 1):
        chosen = jnp.where(index == at, entry, chosen)
    return chosen


ARRIVE = ((1, 3, 2), (3, 2, 0), (0, 3, 1), (2, 0, 1))
WORK = ((1, 3, 2), (2, 0, 3), (0, 3, 1), (2, 0, 1))
SEND = ((2, 3, 1), (2, 3, 0), (1, 0, 3), (1, 0, 2))
PIECES = 4


def iota(shape, axis):
    return lax.broadcasted_iota(jnp.int32, shape, axis)


def fused_kernel(
    tiles,
    offsets_in,
    counts_in,
    mix_in,
    values_in,
    weights_in,
    flow_in,
    choose_in,
    out,
    expected,
    window,
    sorted_weights,
    results,
    scaled,
    chosen,
    cont,
    value,
    base_send,
    base_recv,
    relay_send,
    extra_recv,
    out_send,
    out_recv,
    across_send,
    across_recv,
    over_send,
    over_recv,
    core_send,
    core_recv,
    local_sems,
    offsets,
    counts,
    mix,
    values,
    weights,
    flow,
    choose,
    load_sems,
):
    planes = len(SEND)
    levels, blocks, tile, _ = weights.shape
    rows = values.shape[0]
    near = tiles // planes
    reach = near + blocks - 1
    me = lax.axis_index("skill")
    y = lax.axis_index("grp")
    z = lax.div(me, 4)
    x = lax.rem(lax.div(me, 2), 2)
    core = lax.rem(me, 2)
    last = z + 1 >= planes

    def column(plane):
        return {"skill": plane * 4 + x * 2 + core}

    across = {"skill": z * 4 + (1 - x) * 2 + core}
    over = {"grp": 1 - y}
    partner = {"skill": z * 4 + x * 2 + 1 - core}

    arrays = (
        (values_in, values),
        (mix_in, mix),
        (weights_in, weights),
        (offsets_in, offsets),
        (counts_in, counts),
        (flow_in, flow),
        (choose_in, choose),
    )
    loads = [
        pltpu.make_async_copy(origin, target, load_sems.at[at])
        for at, (origin, target) in enumerate(arrays)
    ]
    for load in loads:
        load.start()

    barrier = pltpu.get_barrier_semaphore()
    for step in range(1, planes):
        pl.semaphore_signal(
            barrier, inc=1, device_id=column(lax.rem(z + step, planes)), device_id_type=MESH
        )
    for other in (across, over, partner):
        pl.semaphore_signal(barrier, inc=1, device_id=other, device_id_type=MESH)

    loads[0].wait()
    loads[1].wait()
    shocks = mix.shape[0]
    both = 2 * rows
    to_row = (iota((both, shocks), 0) % shocks == iota((both, shocks), 1)).astype(jnp.bfloat16)
    to_column = (iota((shocks, both), 1) // 2 % shocks == iota((shocks, both), 0)).astype(jnp.bfloat16)
    down, along = iota((both, both), 0), iota((both, both), 1)
    same = (down // rows == along % 2) & (down % rows // shocks == along // 2 // shocks)

    def spread(part):
        wide = jnp.dot(to_row, part, preferred_element_type=jnp.float32).astype(jnp.bfloat16)
        full = jnp.dot(wide, to_column, preferred_element_type=jnp.float32)
        return jnp.where(same, full, 0.0).astype(jnp.bfloat16)

    parts = [spread(part) for part in split_three(mix[...])]

    def mix_pair(pair, carry):
        block = values[:, :, pl.ds(pl.multiple_of(pair * 2 * tile, 2 * tile), 2 * tile)]
        block = block.reshape(both, 2 * tile)
        total = jnp.dot(parts[2], block, preferred_element_type=jnp.float32)
        total = total + jnp.dot(parts[1], block, preferred_element_type=jnp.float32)
        total = total + jnp.dot(parts[0], block, preferred_element_type=jnp.float32)
        total = total.astype(jnp.bfloat16)
        for a in range(2):
            expected[pair * 2, a] = total[a * rows : (a + 1) * rows, :tile]
            expected[pair * 2 + 1, a] = total[a * rows : (a + 1) * rows, tile:]
        return carry

    lax.fori_loop(0, tiles // 2, mix_pair, 0)
    for r in range(blocks - 1):
        expected[tiles + r] = jnp.zeros(expected.shape[1:], jnp.bfloat16)

    def remote(source, target, send, recv, device):
        return pltpu.make_async_remote_copy(
            src_ref=source,
            dst_ref=target,
            send_sem=send,
            recv_sem=recv,
            device_id=device,
            device_id_type=MESH,
        )

    def base_copy(plane, origin, count):
        return remote(
            expected.at[pl.ds(plane * near, count)],
            window.at[origin, pl.ds(0, count)],
            base_send.at[plane],
            base_recv.at[origin],
            column(plane),
        )

    def each_base(origin, plane, act):
        wide = (plane + 1 >= origin) & (plane + 1 < planes)

        @pl.when(wide)
        def _():
            act(base_copy(plane, origin, reach))

        @pl.when(jnp.logical_not(wide))
        def _():
            act(base_copy(plane, origin, near))

    def relay_copy(origin):
        return remote(
            window.at[origin, pl.ds(0, blocks - 1)],
            window.at[origin, pl.ds(near, blocks - 1)],
            relay_send.at[origin],
            extra_recv.at[origin],
            column(lax.rem(z + planes - 1, planes)),
        )

    def place(side, origin):
        column = (origin * near + lax.rem(x + side, 2) * 2) * tile
        return out.at[:, :, pl.ds(pl.multiple_of(column, 2 * tile), 2 * tile)]

    def out_copy(side, plane, origin):
        return remote(
            results.at[plane, side],
            place(side, origin),
            out_send.at[side, plane],
            out_recv.at[side, origin],
            column(plane),
        )

    def keep_copy(side):
        return pltpu.make_async_copy(results.at[z, side], place(side, z), local_sems.at[side])

    steps = sorted_weights.shape[1]
    part = sorted_weights.shape[2] * (steps // 2) // PIECES
    per_step = sorted_weights.shape[2] // part

    def piece(which, half, index):
        return sorted_weights.at[
            which, half * (steps // 2) + index // per_step, pl.ds(index % per_step * part, part)
        ]

    mine = x * 2 + core
    foreign = (1 - x) * 2 + core

    def across_copy(which, index):
        ref = piece(which, y, index)
        return remote(ref, ref, across_send.at[index], across_recv.at[index], across)

    def over_copy(half, index):
        ref = piece(foreign, half, index)
        return remote(ref, ref, over_send.at[index], over_recv.at[index], over)

    def own_copy(which):
        ref = sorted_weights.at[which]
        return remote(ref, ref, core_send.at[2], core_recv.at[2], partner)

    def half_copy(which, half, index):
        ref = sorted_weights.at[which, pl.ds(half * (steps // 2), steps // 2)]
        return remote(ref, ref, core_send.at[index], core_recv.at[index], partner)

    pl.semaphore_wait(barrier, planes + 2)

    for step in range(planes - 1):
        each_base(z, pick(z, [order[step] for order in SEND]), lambda copy: copy.start())

    for load in loads[2:5]:
        load.wait()
    arrange_weights(
        me, tiles, weights, [offsets[k, 0] for k in range(blocks)], counts[0, 0], sorted_weights.at[mine]
    )
    for index in range(PIECES):
        across_copy(mine, index).start()
    own_copy(mine).start()

    for r in range(reach):
        window[z, r] = expected[z * near + r]

    @pl.when(last)
    def _():
        for step in range(1, planes):
            for r in range(near, reach):
                window[lax.rem(z + step, planes), r] = jnp.zeros(window.shape[2:], jnp.bfloat16)

    def arrive(order):
        origin = pick(z, order)
        each_base(origin, z, lambda copy: copy.wait_recv())

        @pl.when((origin > z) & (z >= 1))
        def _():
            relay_copy(origin).start()

    def hand_on(index):
        across_copy(foreign, index).wait_recv()
        over_copy(y, index).start()

    def compute(origin, side):
        start = pl.multiple_of((origin * 4 + x * 2 + core) * rows, rows)
        flow_here = flow[:, :, pl.ds(start, rows)]
        choose_here = choose[:, :, pl.ds(start, rows)]
        first = lax.rem(x + side, 2) * 2

        def one_tile(t, inner):
            blocks_here = [window[origin, t + r].reshape(2 * rows, tile) for r in range(blocks)]
            one_chunk(
                jnp.concatenate(blocks_here, axis=1),
                flow_here,
                choose_here,
                sorted_weights.at[t],
                scaled,
                chosen,
                cont,
                value,
                levels,
                rows,
            )
            for a in range(2):
                at = pl.ds(pl.multiple_of((t - first) * tile, tile), tile)
                results[origin, side, a, :, at] = value[a].T.astype(jnp.bfloat16)
            return inner

        lax.fori_loop(first, first + 2, one_tile, 0)

    for load in loads[5:]:
        load.wait()
    own_copy(x * 2 + 1 - core).wait_recv()

    def advance(step, carry):
        side = lax.div(step, planes)
        turn = lax.rem(step + planes - 1 + side, planes)
        origin = jnp.where(turn == planes - 1, z, 0)
        for at in range(planes - 1):
            origin = jnp.where(turn == at, pick(z, [order[at] for order in WORK]), origin)

        @pl.when(step == 1)
        def _():
            arrive([order[0] for order in ARRIVE])
            hand_on(0)
            hand_on(1)
            arrive([order[1] for order in ARRIVE])

        @pl.when(step == 2)
        def _():
            hand_on(2)
            hand_on(3)
            half_copy(foreign, y, 0).start()
            arrive([order[2] for order in ARRIVE])

        @pl.when(step == 3)
        def _():
            for index in range(PIECES):
                over_copy(1 - y, index).wait_recv()
            half_copy(foreign, 1 - y, 1).start()

        @pl.when(step == planes)
        def _():
            half_copy((1 - x) * 2 + 1 - core, y, 0).wait_recv()
            half_copy((1 - x) * 2 + 1 - core, 1 - y, 1).wait_recv()

        @pl.when((side == 0) & (origin > z + 1))
        def _():
            relay_copy(origin).wait_recv()

        compute(origin, side)

        @pl.when(origin != z)
        def _():
            out_copy(side, origin, z).start()

        @pl.when(origin == z)
        def _():
            keep_copy(side).start()

        return carry

    lax.fori_loop(0, 2 * planes, advance, 0)

    for side in range(2):
        keep_copy(side).wait()
    own_copy(mine).wait_send()
    half_copy(foreign, y, 0).wait_send()
    half_copy(foreign, 1 - y, 1).wait_send()
    for index in range(PIECES):
        across_copy(mine, index).wait_send()
        over_copy(y, index).wait_send()

    def finish(step, carry):
        plane = lax.rem(z + step, planes)
        each_base(z, plane, lambda copy: copy.wait_send())

        @pl.when((plane > z) & (z >= 1))
        def _():
            relay_copy(plane).wait_send()

        for side in range(2):
            out_copy(side, plane, z).wait_send()
            out_copy(side, plane, plane).wait_recv()
        return carry

    lax.fori_loop(1, planes, finish, 0)


def on_device(value_next, income_matrix, block_weights, block_offset, block_count, asset_next, flow):
    tiles = lax.axis_size("skill")
    planes = len(SEND)
    rows, assets, skills = value_next.shape
    tile = skills // tiles
    levels, blocks = block_weights.shape[1:3]
    hbm = pl.BlockSpec(memory_space=pltpu.HBM)
    dma = pltpu.SemaphoreType.DMA
    back = pl.pallas_call(
        functools.partial(fused_kernel, tiles),
        out_shape=jax.ShapeDtypeStruct((assets, rows, skills), jnp.bfloat16),
        in_specs=[hbm] * 7,
        out_specs=pl.BlockSpec(memory_space=pl.ANY),
        scratch_shapes=[
            pltpu.VMEM((tiles + blocks - 1, assets, rows, tile), jnp.bfloat16),
            pltpu.VMEM((planes, tiles // planes + blocks - 1, assets, rows, tile), jnp.bfloat16),
            pltpu.VMEM((4, tile // STEP, levels * STEP, blocks * tile), jnp.bfloat16),
            pltpu.VMEM((planes, 2, assets, rows, tiles // planes // 2 * tile), jnp.bfloat16),
            pltpu.VMEM((assets, levels, rows), jnp.float32),
            pltpu.VMEM((assets, levels, rows), jnp.int32),
            pltpu.VMEM((2, levels * STEP, assets * rows), jnp.float32),
            pltpu.VMEM((assets, tile, rows), jnp.float32),
            dma((planes,)),
            dma((planes,)),
            dma((planes,)),
            dma((planes,)),
            dma((2, planes)),
            dma((2, planes)),
            dma((PIECES,)),
            dma((PIECES,)),
            dma((PIECES,)),
            dma((PIECES,)),
            dma((3,)),
            dma((3,)),
            dma((2,)),
            pltpu.SMEM((blocks, levels), jnp.int32),
            pltpu.SMEM((1, levels), jnp.int32),
            pltpu.VMEM(income_matrix.shape, jnp.float32),
            pltpu.VMEM(value_next.shape, jnp.bfloat16),
            pltpu.VMEM(block_weights.shape[1:], jnp.bfloat16),
            pltpu.VMEM(flow.shape, jnp.float32),
            pltpu.VMEM(asset_next.shape, jnp.int32),
            dma((7,)),
        ],
        compiler_params=pltpu.CompilerParams(
            collective_id=0, has_side_effects=True, vmem_limit_bytes=67043328
        ),
    )(block_offset[0].T, block_count, income_matrix, value_next, block_weights[0], flow, asset_next)
    return jnp.transpose(back, (1, 0, 2))


def solution(mesh):
    placed = (
        P("skill", "grp", None),
        P("grp", None),
        P("skill", None, None, None, None),
        P("skill", None, None),
        P("skill", None),
        P(),
        P("grp", None, None),
    )

    def body(value_next, income_matrix, *rest):
        whole = value_next.shape[0] % income_matrix.shape[0] == 0
        whole = whole and mesh.shape["skill"] == 4 * len(SEND) and mesh.shape["grp"] == 2
        return (on_device if whole else on_device_split)(value_next, income_matrix, *rest)

    return jax.shard_map(
        body, mesh=mesh, in_specs=placed, out_specs=P("skill", "grp", None), check_vma=False
    )
```
